32 devices in a mesh: groups: 2 (over y), section: 2 (over x), shard: 8 (over z, core).
Axes of the slice: x: 2, y: 2, z: 4, core: 2. Of those that a mesh axis runs over, the one named last changes fastest.
Arguments:
- embed: bfloat16 [1024, 8192], P('groups', 'shard'), parts along dimension 0, may hold values from -6 to 6
- gains: float32 [4, 8192], P('section', 'shard'), may hold values from 0.25 to 1.75
- theta: float32 [4, 8, 2, 64, 8192], P('section', 'groups', None, None, 'shard'), parts along dimension 1, may hold values from -6 to 6
- iterate: float32 [4, 8, 2, 64, 8192], P('section', 'groups', None, None, 'shard'), parts along dimension 1, may hold values from -6 to 6
- residual: float32 [4, 8, 2, 64, 8192], P('section', 'groups', None, None, 'shard'), parts along dimension 1, may hold values from -6 to 6
- direction: float32 [4, 8, 2, 64, 8192], P('section', 'groups', None, None, 'shard'), parts along dimension 1, may hold values from -6 to 6
- token_task: int32 [1024], P('groups'), parts along dimension 0, may hold values from 0 to 3, never falling along the last dimension, each value on 1 to 256 neighbouring positions
- loss_mask: int32 [1024], P('groups'), parts along dimension 0, may hold values 0 or 1
Outputs:
- new_iterate: float32 [4, 8, 2, 64, 8192], P('section', 'groups', None, None, 'shard'), parts along dimension 1
- updated_residual_stream: float32 [4, 8, 2, 64, 8192], P('section', 'groups', None, None, 'shard'), parts along dimension 1
- new_direction: float32 [4, 8, 2, 64, 8192], P('section', 'groups', None, None, 'shard'), parts along dimension 1
The draws below stay inside these ranges and needn't reach their ends.
There are 2 independent parts, one for each index of `groups`. The reference program is written for one: setup_inputs(seed, part) draws one part's arguments, and reference() takes and returns one part's arrays. A program takes and returns all parts, laid end to end along the dimension named above; an argument that names none is the same for every part. Nothing has to cross between parts.
Inputs may be any that keep to these rules, and one draw needn't show every extreme that they name: `token_task`: tokens of one task stand together, tasks in increasing order; each task has 1 to 256 tokens and one has exactly 256.
All inputs are finite; a program needn't handle non-finite values.
Results may differ from the reference program's by a relative error of at most 0.0003.
Values sent between devices are 32-bit elements; how exact they have to be, the bound alone decides.
A program may use at most 128 MiB of HBM per device.

```python
import math
import jax
import jax.numpy as jnp
import numpy as np
from jax import lax

D = 8192
ADAPTER_RANK = 64
TASKS = 4
TOKENS = 512
MOST = 256
LAYERS = 4


def with_ends(values, stream_key, smallest, largest):
    spot = [jax.random.randint(jax.random.fold_in(stream_key, axis), (), 0, length) for axis, length in enumerate(values.shape)]
    longest = values.shape.index(max(values.shape))
    beside = spot[:longest] + [(spot[longest] + 1) % values.shape[longest]] + spot[longest + 1:]
    return values.at[tuple(spot)].set(smallest).at[tuple(beside)].set(largest)


def shard_levels(stream_key, dims, shards, smallest, high):
    def one(position, blocks):
        steps = jax.random.uniform(jax.random.fold_in(jax.random.fold_in(stream_key, 6), position), (blocks,), jnp.float32, smallest / len(shards), high / len(shards))
        return jnp.repeat(jnp.exp(steps), dims[position] // blocks).reshape((-1,) + (1,) * (len(dims) - position - 1))

    level = one(*shards[0])
    for cut in shards[1:]:
        level = level * one(*cut)
    return level


def length_profile(count, total, limit, skew):
    weights = [(1 << 20) // math.isqrt(grade ** skew) + 1 for grade in range(2, count + 1)]
    spare, counts = total - limit - (count - 1), [1] * (count - 1)
    while spare > 0:
        candidates = [i for i in range(count - 1) if counts[i] < limit]
        pool, remaining = sum([weights[i] for i in candidates]), spare
        for i in candidates:
            extra = min(limit - counts[i], max(1, remaining * weights[i] // pool), spare)
            counts[i] = counts[i] + extra
            spare = spare - extra
    return np.array([limit] + counts)


def uneven(key, amount, total, most, slope):
    if amount == 2:
        one = jax.random.randint(key, (), max(1, total - most), min(most, total - 1) + 1)
        return jnp.stack([one, total - one])
    lengths = jnp.asarray(length_profile(amount, total, most, slope), jnp.int32)
    pairs = (amount - 1) // 2
    giver, taker = lengths[1:1 + 2 * pairs:2], lengths[2:2 + 2 * pairs:2]
    margin = jnp.minimum(giver - 1, most - taker)
    shifted = jax.random.randint(jax.random.fold_in(key, 1), (pairs,), 0, 1 << 20) % (margin + 1)
    lengths = lengths.at[1:1 + 2 * pairs:2].set(giver - shifted).at[2:2 + 2 * pairs:2].set(taker + shifted)
    return lengths[jax.random.permutation(jax.random.fold_in(key, 2), amount)]


def normal_values(rng, shape, scale, bound, shards=(), kind=jnp.bfloat16):
    gain = shard_levels(rng, shape, shards, -0.22, 0.18) if shards else 1.0
    array = jax.random.normal(rng, shape, jnp.float32) * scale * gain
    return jnp.minimum(jnp.maximum(array, -bound), bound).astype(kind)


def setup_inputs(seed: int = 0, part: int = 0) -> dict:
    key_list = jax.random.split(jax.random.key(seed), 9)
    part_splits = jax.random.split(jax.random.fold_in(key_list[8], part), 9)
    embed = normal_values(part_splits[0], (TOKENS, D), 1.0, 6.0, ((1, 8),))
    gains = jnp.clip(1.0 + 0.15 * jax.random.normal(key_list[1], (LAYERS, D), jnp.float32), 0.25, 1.75)
    theta = normal_values(part_splits[2], (LAYERS, TASKS, 2, ADAPTER_RANK, D), 1.0, 6.0, ((0, 2), (4, 8)), jnp.float32)
    iterate = normal_values(part_splits[3], (LAYERS, TASKS, 2, ADAPTER_RANK, D), 1.0, 6.0, ((0, 2), (4, 8)), jnp.float32)
    residual = normal_values(part_splits[4], (LAYERS, TASKS, 2, ADAPTER_RANK, D), 1.0, 6.0, ((0, 2), (4, 8)), jnp.float32)
    direction = normal_values(part_splits[5], (LAYERS, TASKS, 2, ADAPTER_RANK, D), 1.0, 6.0, ((0, 2), (4, 8)), jnp.float32)
    token_task = jnp.searchsorted(jnp.cumsum(uneven(part_splits[6], TASKS, TOKENS, MOST, 2)), jnp.arange(TOKENS), side="right").astype(jnp.int32)
    loss_mask = with_ends((jax.random.randint(part_splits[7], (TOKENS,), 0, 4) < 3).astype(jnp.int32), jax.random.fold_in(part_splits[7], 1), 0, 1)
    return dict(embed=embed, gains=gains, theta=theta, iterate=iterate, residual=residual, direction=direction, token_task=token_task, loss_mask=loss_mask)


EPSILON = 1e-05
ADAPTER_SCALE = 0.5
DAMPING_FACTOR = 0.5
HIGH = lax.Precision.HIGHEST

def network(parameters, embed, gains, onehot):
    width = embed.shape[1]
    down_scale = width ** (-0.5)
    up_projection_scale = ADAPTER_SCALE * parameters.shape[3] ** (-0.5)
    hidden = embed.astype(jnp.float32)
    for layer_index in range(parameters.shape[0]):
        recip = 1.0 / jnp.sqrt(lax.optimization_barrier(jnp.sum(hidden * hidden, axis=-1)) / width + EPSILON)
        normed = hidden * gains[layer_index] * recip[:, None]
        expanded = jnp.einsum('td,krd->tkr', normed, parameters[layer_index, :, 0], precision=HIGH)
        lowrank = lax.optimization_barrier(jnp.sum(expanded * onehot[:, :, None], axis=1)) * down_scale
        picked = onehot[:, :, None] * lowrank[:, None, :]
        hidden = hidden + up_projection_scale * jnp.einsum('tkr,krd->td', picked, parameters[layer_index, :, 1], precision=HIGH)
    return hidden

def reference(embed, gains, theta, iterate, residual, direction, token_task, loss_mask):
    onehot = (token_task[:, None] == jnp.arange(theta.shape[1], dtype=jnp.int32)[None, :]).astype(jnp.float32)

    def mapping(parameters):
        return network(parameters, embed, gains, onehot)
    result, tangent = jax.jvp(mapping, (theta,), (direction,))
    weighted = tangent * loss_mask.astype(jnp.float32)[:, None]
    result_again, pullback = jax.vjp(mapping, theta)
    curved = pullback(weighted)[0]
    product = curved + DAMPING_FACTOR * direction
    squared_old = jnp.sum(residual * residual)
    alpha = squared_old / jnp.sum(direction * product)
    new_iterate = iterate + alpha * direction
    updated_residual_stream = residual - alpha * product
    squared_new = jnp.sum(updated_residual_stream * updated_residual_stream)
    new_direction = updated_residual_stream + squared_new / squared_old * direction
    return (new_iterate, updated_residual_stream, new_direction)
```

```python
import functools

import jax
import jax.numpy as jnp
from jax import lax
from jax.experimental import pallas as pl
from jax.experimental.pallas import tpu as pltpu
from jax.sharding import PartitionSpec as P

D = 8192
ADAPTER_RANK = 64
EPSILON = 1e-05
ADAPTER_SCALE = 0.5
DAMPING_FACTOR = 0.5
PREC = lax.Precision.HIGH
DOWN = D ** (-0.5)
UP = ADAPTER_SCALE * ADAPTER_RANK ** (-0.5)
MESH = pl.DeviceIdType.MESH


def reduce_kernel(sections, shards, has_big, has_small, *refs):
    refs = list(refs)
    big = refs.pop(0) if has_big else None
    small = refs.pop(0) if has_small else None
    out = refs.pop(0) if has_big else None
    small_out = refs.pop(0) if has_small else None
    if has_big:
        landed, send1, recv1, send2, recv2 = refs[:5]
        refs = refs[5:]
    if has_small:
        small_landed, send3, recv3 = refs[:3]
    count = sections * shards
    me = lax.axis_index("section") * shards + lax.axis_index("shard")

    def spot(index):
        return {"section": lax.div(index, shards), "shard": lax.rem(index, shards)}

    def ahead(step):
        return lax.rem(me + step, count)

    barrier = pltpu.get_barrier_semaphore()
    for step in range(1, count):
        pl.semaphore_signal(barrier, inc=1, device_id=spot(ahead(step)), device_id_type=MESH)
    pl.semaphore_wait(barrier, count - 1)
    first, second, tiny = [], [], []
    for step in range(1, count):
        target = ahead(step)
        if has_big:
            first.append(
                pltpu.make_async_remote_copy(
                    src_ref=big.at[target],
                    dst_ref=landed.at[step],
                    send_sem=send1.at[step],
                    recv_sem=recv1.at[step],
                    device_id=spot(target),
                    device_id_type=MESH,
                )
            )
            first[-1].start()
        if has_small:
            tiny.append(
                pltpu.make_async_remote_copy(
                    src_ref=small,
                    dst_ref=small_landed.at[step],
                    send_sem=send3.at[step],
                    recv_sem=recv3.at[step],
                    device_id=spot(target),
                    device_id_type=MESH,
                )
            )
            tiny[-1].start()
    if has_big:
        total = big[me]
        for step in range(1, count):
            first[step - 1].wait_recv()
            total = total + landed[step]
        out[me] = total
        for step in range(1, count):
            second.append(
                pltpu.make_async_remote_copy(
                    src_ref=out.at[me],
                    dst_ref=out.at[me],
                    send_sem=send2.at[step],
                    recv_sem=recv2.at[step],
                    device_id=spot(ahead(step)),
                    device_id_type=MESH,
                )
            )
            second[-1].start()
    if has_small:
        total = small[...]
        for step in range(1, count):
            tiny[step - 1].wait_recv()
            total = total + small_landed[step]
        small_out[...] = total
        for copy in tiny:
            copy.wait_send()
    if has_big:
        for copy in first:
            copy.wait_send()
        for step in range(1, count):
            source = lax.rem(me + count - step, count)
            pltpu.make_async_remote_copy(
                src_ref=out.at[source],
                dst_ref=out.at[source],
                send_sem=send2.at[step],
                recv_sem=recv2.at[step],
                device_id=spot(ahead(step)),
                device_id_type=MESH,
            ).wait_recv()
        for copy in second:
            copy.wait_send()


def total_over(big, small, collective_id):
    sections, shards = lax.axis_size("section"), lax.axis_size("shard")
    count = sections * shards
    rows = 8 * count if big is None else big.shape[0]
    if count > 16 or rows % (8 * count):
        given = tuple(part for part in (big, small) if part is not None)
        done = list(lax.psum(given, ("section", "shard")))
        return (
            done.pop(0) if big is not None else None,
            done.pop(0) if small is not None else None,
        )
    args, outs, scratch = [], [], []
    dma = pltpu.SemaphoreType.DMA((count,))
    if big is not None:
        shape = (count, rows // count, 128)
        args.append(big.reshape(shape))
        outs.append(jax.ShapeDtypeStruct(shape, jnp.float32))
        scratch += [pltpu.VMEM(shape, jnp.float32), dma, dma, dma, dma]
    if small is not None:
        args.append(small)
        outs.append(jax.ShapeDtypeStruct(small.shape, jnp.float32))
        scratch += [pltpu.VMEM((count,) + small.shape, jnp.float32), dma, dma]
    done = pl.pallas_call(
        functools.partial(reduce_kernel, sections, shards, big is not None, small is not None),
        out_shape=tuple(outs),
        in_specs=[pl.BlockSpec(memory_space=pltpu.VMEM)] * len(args),
        out_specs=tuple([pl.BlockSpec(memory_space=pltpu.VMEM)] * len(outs)),
        scratch_shapes=scratch,
        name="total_over_%d" % collective_id,
        compiler_params=pltpu.CompilerParams(collective_id=collective_id, has_side_effects=True),
    )(*args)
    done = list(done)
    return (
        done.pop(0).reshape(big.shape) if big is not None else None,
        done.pop(0) if small is not None else None,
    )


def scalars_tile(*values):
    row = jnp.stack(values)
    return jnp.pad(row[:, None], ((0, 8 - len(values)), (0, 127)))


def dot_t(a, b):
    return lax.dot_general(a, b, (((1,), (1,)), ((), ())), precision=PREC)


def dot_n(a, b):
    return lax.dot_general(a, b, (((1,), (0,)), ((), ())), precision=PREC)


def dot_rows(a, b):
    return lax.dot_general(a, b, (((0,), (0,)), ((), ())), precision=PREC)


def body(embed, gains, theta, iterate, residual, direction, token_task, loss_mask):
    section = lax.axis_index("section")
    sections = lax.axis_size("section")
    here, tasks = theta.shape[0], theta.shape[1]
    rank = theta.shape[3]
    layers = here * sections
    tokens, width = embed.shape
    part = width // sections
    wide = tasks * rank
    half = tokens // 2
    onehot = (token_task[:, None] == jnp.arange(tasks, dtype=jnp.int32)[None, :]).astype(
        jnp.float32
    )
    weights = loss_mask.astype(jnp.float32)

    def pick(values):
        return sum(
            values[:, k * rank : (k + 1) * rank] * onehot[:, k : k + 1] for k in range(tasks)
        )

    def spread(values):
        return jnp.concatenate([values * onehot[:, k : k + 1] for k in range(tasks)], axis=1)

    def columns(value, block):
        return lax.dynamic_slice_in_dim(value, block * part, part, value.ndim - 1)

    local = {}
    for j in range(here):
        for side in range(2):
            both = jnp.concatenate(
                [theta[j, :, side].reshape(wide, width), direction[j, :, side].reshape(wide, width)]
            )
            local[j, side] = both * gains[j] if side == 0 else both
    order = [(0, 1)] + [(j, side) for j in range(1, here) for side in range(2)] + [(0, 0)]
    mats = {}
    for j, side in order:
        choices = [columns(local[j, side], section)]
        for k in range(1, sections):
            choices.append(
                lax.ppermute(
                    columns(local[j, side], lax.rem(section + k, sections)),
                    "section",
                    [(s, (s + k) % sections) for s in range(sections)],
                )
            )
        for q in range(sections):
            away = lax.rem(section + sections - q, sections)
            mats[q * here + j, side] = lax.select_n(away, *choices)

    embedded = embed.astype(jnp.float32)
    hidden = columns(embedded, section)
    moving = None
    saved = []
    for layer in range(layers):
        squares = jnp.sum(hidden * hidden, axis=-1)
        if layer == 0:
            first = dot_t(embedded, local[0, 0])
            raw = jnp.concatenate([pick(first[:, :wide]), pick(first[:, wide:])], axis=1)
            raw = jnp.where(section == 0, raw, 0.0)
            products = jnp.zeros_like(squares)
        else:
            first = dot_t(hidden, mats[layer, 0])
            extra = dot_t(moving, mats[layer, 0][:wide])
            raw = jnp.concatenate([pick(first[:, :wide]), pick(first[:, wide:] + extra)], axis=1)
            products = jnp.sum(hidden * moving, axis=-1)
        small = jnp.concatenate([squares.reshape(-1, 128), products.reshape(-1, 128)])
        raw, small = total_over(raw, small, 0)
        squares = small[: tokens // 128].reshape(tokens)
        products = small[tokens // 128 :].reshape(tokens)
        recip = 1.0 / jnp.sqrt(squares / D + EPSILON)
        drift = -(recip**3) * products / D
        low = raw[:, :rank] * (DOWN * recip)[:, None]
        lowmove = (raw[:, rank:] * recip[:, None] + raw[:, :rank] * drift[:, None]) * DOWN
        saved.append((hidden, recip, low))
        spread_low = spread(UP * low)
        up = dot_n(jnp.concatenate([spread(UP * lowmove), spread_low], axis=1), mats[layer, 1])
        hidden = hidden + dot_n(spread_low, mats[layer, 1][:wide])
        moving = up if moving is None else moving + up

    cot = moving * weights[:, None]
    scalars = scalars_tile(
        jnp.sum(cot * moving), jnp.sum(direction * direction), jnp.sum(residual * residual)
    )
    grads = {}
    for layer in reversed(range(layers)):
        hidden, recip, low = saved[layer]
        partial = pick(dot_t(cot, mats[layer, 1][:wide])) * UP
        packed = jnp.concatenate([partial[:half], partial[half:]], axis=1)
        if layer == layers - 1:
            packed, summed = total_over(packed, scalars, 1)
            squared_old = summed[2, 0]
            alpha = squared_old / (summed[0, 0] + DAMPING_FACTOR * summed[1, 0])
        else:
            packed, _ = total_over(packed, None, 2)
        grads[layer, 1] = dot_rows(spread(UP * low), cot)
        low_cot = jnp.concatenate([packed[:, :rank], packed[:, rank:]])
        spread_cot = spread(low_cot * (DOWN * recip)[:, None])
        if layer == 0:
            first_down = dot_rows(spread_cot, embedded)
        else:
            grads[layer, 0] = dot_rows(spread_cot, hidden)
            pull = recip * recip * jnp.sum(low_cot * low, axis=-1) / D
            cot = cot + dot_n(spread_cot, mats[layer, 0][:wide]) - pull[:, None] * hidden

    product = []
    for j in range(here):
        for side in range(2):
            blocks = []
            candidates = []
            for q in range(sections):
                layer = q * here + j
                if layer == 0 and side == 0:
                    candidates.append(first_down)
                    continue
                parts = []
                for m in range(sections):
                    if m == q:
                        parts.append(grads[layer, side])
                    else:
                        parts.append(lax.ppermute(grads[layer, side], "section", [(m, q)]))
                candidates.append(jnp.concatenate(parts, axis=1))
            full = lax.select_n(section, *candidates)
            product.append(full * gains[j] if side == 0 else full)
    gradient = jnp.stack(product).reshape(here, 2, tasks, rank, width).transpose(0, 2, 1, 3, 4)
    product = gradient + DAMPING_FACTOR * direction
    new_iterate = iterate + alpha * direction
    updated_residual_stream = residual - alpha * product
    _, summed = total_over(
        None, scalars_tile(jnp.sum(updated_residual_stream * updated_residual_stream)), 3
    )
    new_direction = updated_residual_stream + summed[0, 0] / squared_old * direction
    return (new_iterate, updated_residual_stream, new_direction)


def solution(mesh):
    spec = P("section", "groups", None, None, "shard")
    return jax.shard_map(
        body,
        mesh=mesh,
        in_specs=(
            P("groups", "shard"),
            P("section", "shard"),
            spec,
            spec,
            spec,
            spec,
            P("groups"),
            P("groups"),
        ),
        out_specs=(spec, spec, spec),
        check_vma=False,
    )
```

```python
import functools

import jax
import jax.numpy as jnp
from jax import lax
from jax.experimental import pallas as pl
from jax.experimental.pallas import tpu as pltpu
from jax.sharding import PartitionSpec as P

D = 8192
ADAPTER_RANK = 64
EPSILON = 1e-05
ADAPTER_SCALE = 0.5
DAMPING_FACTOR = 0.5
PREC = lax.Precision.HIGH
DOWN = D ** (-0.5)
UP = ADAPTER_SCALE * ADAPTER_RANK ** (-0.5)
MESH = pl.DeviceIdType.MESH


def reduce_kernel(sections, shards, has_big, has_small, *refs):
    refs = list(refs)
    big = refs.pop(0) if has_big else None
    small = refs.pop(0) if has_small else None
    out = refs.pop(0) if has_big else None
    small_out = refs.pop(0) if has_small else None
    if has_big:
        landed, send1, recv1, send2, recv2 = refs[:5]
        refs = refs[5:]
    if has_small:
        small_landed, send3, recv3 = refs[:3]
    count = sections * shards
    me = lax.axis_index("section") * shards + lax.axis_index("shard")

    def spot(index):
        return {"section": lax.div(index, shards), "shard": lax.rem(index, shards)}

    def ahead(step):
        return lax.rem(me + step, count)

    barrier = pltpu.get_barrier_semaphore()
    for step in range(1, count):
        pl.semaphore_signal(barrier, inc=1, device_id=spot(ahead(step)), device_id_type=MESH)
    pl.semaphore_wait(barrier, count - 1)
    first, second, tiny = [], [], []
    for step in range(1, count):
        target = ahead(step)
        if has_big:
            first.append(
                pltpu.make_async_remote_copy(
                    src_ref=big.at[target],
                    dst_ref=landed.at[step],
                    send_sem=send1.at[step],
                    recv_sem=recv1.at[step],
                    device_id=spot(target),
                    device_id_type=MESH,
                )
            )
            first[-1].start()
        if has_small:
            tiny.append(
                pltpu.make_async_remote_copy(
                    src_ref=small,
                    dst_ref=small_landed.at[step],
                    send_sem=send3.at[step],
                    recv_sem=recv3.at[step],
                    device_id=spot(target),
                    device_id_type=MESH,
                )
            )
            tiny[-1].start()
    if has_big:
        total = big[me]
        for step in range(1, count):
            first[step - 1].wait_recv()
            total = total + landed[step]
        out[me] = total
        for step in range(1, count):
            second.append(
                pltpu.make_async_remote_copy(
                    src_ref=out.at[me],
                    dst_ref=out.at[me],
                    send_sem=send2.at[step],
                    recv_sem=recv2.at[step],
                    device_id=spot(ahead(step)),
                    device_id_type=MESH,
                )
            )
            second[-1].start()
    if has_small:
        total = small[...]
        for step in range(1, count):
            tiny[step - 1].wait_recv()
            total = total + small_landed[step]
        small_out[...] = total
        for copy in tiny:
            copy.wait_send()
    if has_big:
        for copy in first:
            copy.wait_send()
        for step in range(1, count):
            source = lax.rem(me + count - step, count)
            pltpu.make_async_remote_copy(
                src_ref=out.at[source],
                dst_ref=out.at[source],
                send_sem=send2.at[step],
                recv_sem=recv2.at[step],
                device_id=spot(ahead(step)),
                device_id_type=MESH,
            ).wait_recv()
        for copy in second:
            copy.wait_send()


def total_over(big, small, collective_id):
    sections, shards = lax.axis_size("section"), lax.axis_size("shard")
    count = sections * shards
    rows = 8 * count if big is None else big.shape[0]
    if count > 16 or rows % (8 * count):
        given = tuple(part for part in (big, small) if part is not None)
        done = list(lax.psum(given, ("section", "shard")))
        return (
            done.pop(0) if big is not None else None,
            done.pop(0) if small is not None else None,
        )
    args, outs, scratch = [], [], []
    dma = pltpu.SemaphoreType.DMA((count,))
    if big is not None:
        shape = (count, rows // count, 128)
        args.append(big.reshape(shape))
        outs.append(jax.ShapeDtypeStruct(shape, jnp.float32))
        scratch += [pltpu.VMEM(shape, jnp.float32), dma, dma, dma, dma]
    if small is not None:
        args.append(small)
        outs.append(jax.ShapeDtypeStruct(small.shape, jnp.float32))
        scratch += [pltpu.VMEM((count,) + small.shape, jnp.float32), dma, dma]
    done = pl.pallas_call(
        functools.partial(reduce_kernel, sections, shards, big is not None, small is not None),
        out_shape=tuple(outs),
        in_specs=[pl.BlockSpec(memory_space=pltpu.VMEM)] * len(args),
        out_specs=tuple([pl.BlockSpec(memory_space=pltpu.VMEM)] * len(outs)),
        scratch_shapes=scratch,
        name="total_over_%d" % collective_id,
        cost_estimate=pl.CostEstimate(flops=0, bytes_accessed=50_000_000, transcendentals=0),
        compiler_params=pltpu.CompilerParams(collective_id=collective_id, has_side_effects=True),
    )(*args)
    done = list(done)
    return (
        done.pop(0).reshape(big.shape) if big is not None else None,
        done.pop(0) if small is not None else None,
    )


def scalars_tile(*values):
    row = jnp.stack(values)
    return jnp.pad(row[:, None], ((0, 8 - len(values)), (0, 127)))


def contract(a, b, axis_a, axis_b, split):
    dims = (((axis_a,), (axis_b,)), ((), ()))
    if not split:
        return lax.dot_general(a, b, dims, precision=PREC)

    def halves(x):
        high = x.astype(jnp.bfloat16)
        return high, (x - high.astype(jnp.float32)).astype(jnp.bfloat16)

    def mul(x, y):
        return lax.dot_general(x, y, dims, preferred_element_type=jnp.float32)

    (ah, al), (bh, bl) = halves(a), halves(b)
    return mul(ah, bh) + (mul(ah, bl) + mul(al, bh))


def pick(values, mask, rank):
    masked = values * mask
    count = masked.shape[1] // rank
    return sum(masked[:, k * rank : (k + 1) * rank] for k in range(count))


def spread(values, mask):
    count = mask.shape[1] // values.shape[1]
    return jnp.concatenate([values] * count, axis=1) * mask


def scale_low(raw, stats):
    rank = raw.shape[1] // 2
    recip = 1.0 / jnp.sqrt(stats[:, 0:1] / D + EPSILON)
    drift = -(recip * recip * recip) * stats[:, 1:2] / D
    low = raw[:, :rank] * (DOWN * recip)
    lowmove = (raw[:, rank:] * recip + raw[:, :rank] * drift) * DOWN
    return recip, low, lowmove


def step_up(split, raw, stats, mask, hidden, moving, up):
    wide = mask.shape[1]
    recip, low, lowmove = scale_low(raw, stats)
    spread_low = spread(UP * low, mask)
    fresh = hidden + contract(spread_low, up[:wide], 1, 0, split)
    move = contract(spread(UP * lowmove, mask), up[:wide], 1, 0, split)
    move = move + contract(spread_low, up[wide:], 1, 0, split)
    if moving is not None:
        move = move + moving
    return fresh, move, recip, low


def forward_step(has_moving, split, raw, stats, mask, hidden, *rest):
    moving, (up, down) = (rest[0], rest[1:]) if has_moving else (None, rest)
    wide, rank = mask.shape[1], raw.shape[1] // 2
    fresh, move, recip, low = step_up(split, raw, stats, mask, hidden, moving, up)
    first = contract(fresh, down[:wide], 1, 1, split)
    second = contract(fresh, down[wide:], 1, 1, split) + contract(move, down[:wide], 1, 1, split)
    raw_next = jnp.concatenate([pick(first, mask, rank), pick(second, mask, rank)], axis=1)
    squares = jnp.sum(fresh * fresh, axis=1, keepdims=True)
    products = jnp.sum(fresh * move, axis=1, keepdims=True)
    return fresh, move, recip, low, raw_next, jnp.concatenate([squares, products], axis=1)


def last_step(split, raw, stats, mask, weights, hidden, moving, up):
    wide, rank = mask.shape[1], raw.shape[1] // 2
    _, move, recip, low = step_up(split, raw, stats, mask, hidden, moving, up)
    cot = move * weights
    partial = pick(contract(cot, up[:wide], 1, 1, split), mask, rank) * UP
    return cot, recip, low, partial, jnp.sum(cot * move, axis=1, keepdims=True)


def backward_step(split, low_cot, low, recip, mask, cot, hidden, down, up_before):
    rank = low.shape[1]
    grad_up = contract(spread(UP * low, mask), cot, 0, 0, split)
    spread_cot = spread(low_cot * (DOWN * recip), mask)
    grad_down = contract(spread_cot, hidden, 0, 0, split)
    pull = recip * recip * jnp.sum(low_cot * low, axis=1, keepdims=True) / D
    fresh = cot + contract(spread_cot, down, 1, 0, split) - pull * hidden
    partial = pick(contract(fresh, up_before, 1, 1, split), mask, rank) * UP
    return grad_up, grad_down, fresh, partial


def run_local(function, part, shapes, *args):
    if part % 128:
        return function(False, *args)

    def kernel(*refs):
        values = function(True, *[ref[...] for ref in refs[: len(args)]])
        for ref, value in zip(refs[len(args) :], values):
            ref[...] = value

    vmem = pl.BlockSpec(memory_space=pltpu.VMEM)
    return pl.pallas_call(
        kernel,
        out_shape=tuple(jax.ShapeDtypeStruct(shape, jnp.float32) for shape in shapes),
        in_specs=[vmem] * len(args),
        out_specs=tuple([vmem] * len(shapes)),
        cost_estimate=pl.CostEstimate(flops=0, bytes_accessed=15_000_000, transcendentals=0),
        compiler_params=pltpu.CompilerParams(vmem_limit_bytes=40 * 1024 * 1024),
    )(*args)


def body(embed, gains, theta, iterate, residual, direction, token_task, loss_mask):
    section = lax.axis_index("section")
    sections = lax.axis_size("section")
    here, tasks = theta.shape[0], theta.shape[1]
    rank = theta.shape[3]
    layers = here * sections
    tokens, width = embed.shape
    part = width // sections
    wide = tasks * rank
    half = tokens // 2
    onehot = (token_task[:, None] == jnp.arange(tasks, dtype=jnp.int32)[None, :]).astype(
        jnp.float32
    )
    mask = jnp.repeat(onehot, rank, axis=1)
    weights = loss_mask.astype(jnp.float32)[:, None]

    def columns(value, block):
        return lax.dynamic_slice_in_dim(value, block * part, part, value.ndim - 1)

    local = {}
    for j in range(here):
        for side in range(2):
            both = jnp.concatenate(
                [theta[j, :, side].reshape(wide, width), direction[j, :, side].reshape(wide, width)]
            )
            local[j, side] = both * gains[j][None, :] if side == 0 else both

    def fetch(layer, side, after):
        owner, j = layer // here, layer % here
        got = None
        for k in range(1, sections):
            target = (owner + k) % sections
            piece = local[j, side][:, target * part : (target + 1) * part]
            if after is not None:
                piece, _ = lax.optimization_barrier((piece, after))
            came = lax.ppermute(piece, "section", [(owner, target)])
            got = came if got is None else got + came
        own = local[j, side][:, owner * part : (owner + 1) * part]
        return own if got is None else jnp.where(section == owner, own, got)

    mats = {}

    def fetch_wave(wave, after):
        for layer in range(layers):
            for side in range(2):
                turn = max(0, layer + side - (2 if layer >= here else 1))
                if (layer, side) != (0, 0) and min(turn, layers - 2) == wave:
                    mats[layer, side] = fetch(layer, side, after)

    embedded = embed.astype(jnp.float32)
    hidden = columns(embedded, section)
    moving = None
    saved = []
    fetch_wave(0, None)
    first = contract(embedded, local[0, 0], 1, 1, False)
    raw = jnp.concatenate(
        [pick(first[:, :wide], mask, rank), pick(first[:, wide:], mask, rank)], axis=1
    )
    raw = jnp.where(section == 0, raw, 0.0)
    squares = jnp.sum(hidden * hidden, axis=1, keepdims=True)
    stats = jnp.concatenate([squares, jnp.zeros_like(squares)], axis=1)
    square, tall = (tokens, part), (tokens, rank)
    one, two = (tokens, 1), (tokens, 2)
    for layer in range(layers):
        small = stats.T.reshape(8, -1)
        raw, small = total_over(raw, small, 0)
        stats = small.reshape(2, tokens).T
        if layer < layers - 1:
            if layer < layers - 2:
                fetch_wave(layer + 1, raw)
            given = (raw, stats, mask, hidden) + (() if moving is None else (moving,))
            fresh, move, recip, low, raw, stats = run_local(
                functools.partial(forward_step, moving is not None),
                part,
                (square, square, one, tall, (tokens, 2 * rank), two),
                *given,
                mats[layer, 1],
                mats[layer + 1, 0],
            )
            saved.append((hidden, recip, low))
            hidden, moving = fresh, move
        else:
            cot, recip, low, partial, curved = run_local(
                last_step,
                part,
                (square, one, tall, tall, one),
                raw, stats, mask, weights, hidden, moving, mats[layer, 1],
            )
            saved.append((hidden, recip, low))

    scalars = scalars_tile(
        jnp.sum(curved), jnp.sum(direction * direction), jnp.sum(residual * residual)
    )
    came = {}

    def send_home(layer, side, value):
        owner = layer // here
        parts = []
        for m in range(sections):
            parts.append(value if m == owner else lax.ppermute(value, "section", [(m, owner)]))
        came[layer, side] = parts

    for layer in reversed(range(layers)):
        hidden, recip, low = saved[layer]
        packed = jnp.concatenate([partial[:half], partial[half:]], axis=1)
        if layer == layers - 1:
            packed, summed = total_over(packed, scalars, 1)
            squared_old = summed[2, 0]
            alpha = squared_old / (summed[0, 0] + DAMPING_FACTOR * summed[1, 0])
        else:
            if layer + 2 < layers:
                packed, came[layer + 2, 0], came[layer + 2, 1] = lax.optimization_barrier(
                    (packed, came[layer + 2, 0], came[layer + 2, 1])
                )
            if layer == 0:
                send_home(0, 1, contract(spread(UP * low, mask), cot, 0, 0, False))
            packed, _ = total_over(packed, None, 2)
        low_cot = jnp.concatenate([packed[:, :rank], packed[:, rank:]])
        if layer == 0:
            spread_cot = spread(low_cot * (DOWN * recip), mask)
            first_down = contract(spread_cot, embedded, 0, 0, False)
        else:
            grad_up, grad_down, cot, partial = run_local(
                backward_step,
                part,
                ((wide, part), (wide, part), square, tall),
                low_cot, low, recip, mask, cot, hidden, mats[layer, 0][:wide], mats[layer - 1, 1][:wide],
            )
            send_home(layer, 0, grad_down)
            send_home(layer, 1, grad_up)

    product = []
    for j in range(here):
        for side in range(2):
            candidates = []
            for q in range(sections):
                layer = q * here + j
                if layer == 0 and side == 0:
                    candidates.append(first_down)
                else:
                    candidates.append(jnp.concatenate(came[layer, side], axis=1))
            full = lax.select_n(section, *candidates)
            product.append(full * gains[j][None, :] if side == 0 else full)
    gradient = jnp.stack(product).reshape(here, 2, tasks, rank, width).transpose(0, 2, 1, 3, 4)
    product = gradient + DAMPING_FACTOR * direction
    new_iterate = iterate + alpha * direction
    updated_residual_stream = residual - alpha * product
    _, summed = total_over(
        None, scalars_tile(jnp.sum(updated_residual_stream * updated_residual_stream)), 3
    )
    new_direction = updated_residual_stream + summed[0, 0] / squared_old * direction
    return (new_iterate, updated_residual_stream, new_direction)


def solution(mesh):
    spec = P("section", "groups", None, None, "shard")
    return jax.shard_map(
        body,
        mesh=mesh,
        in_specs=(
            P("groups", "shard"),
            P("section", "shard"),
            spec,
            spec,
            spec,
            spec,
            P("groups"),
            P("groups"),
        ),
        out_specs=(spec, spec, spec),
        check_vma=False,
    )
```

```python
import functools

import jax
import jax.numpy as jnp
from jax import lax
from jax.experimental import pallas as pl
from jax.experimental.pallas import tpu as pltpu
from jax.sharding import PartitionSpec as P

D = 8192
ADAPTER_RANK = 64
EPSILON = 1e-05
ADAPTER_SCALE = 0.5
DAMPING_FACTOR = 0.5
PREC = lax.Precision.HIGH
DOWN = D ** (-0.5)
UP = ADAPTER_SCALE * ADAPTER_RANK ** (-0.5)
MESH = pl.DeviceIdType.MESH


def reduce_kernel(sections, shards, has_big, has_small, *refs):
    refs = list(refs)
    big = refs.pop(0) if has_big else None
    small = refs.pop(0) if has_small else None
    out = refs.pop(0) if has_big else None
    small_out = refs.pop(0) if has_small else None
    if has_big:
        landed, send1, recv1, send2, recv2 = refs[:5]
        refs = refs[5:]
    if has_small:
        small_landed, send3, recv3 = refs[:3]
    count = sections * shards
    me = lax.axis_index("section") * shards + lax.axis_index("shard")

    def spot(index):
        return {"section": lax.div(index, shards), "shard": lax.rem(index, shards)}

    def ahead(step):
        return lax.rem(me + step, count)

    barrier = pltpu.get_barrier_semaphore()
    for step in range(1, count):
        pl.semaphore_signal(barrier, inc=1, device_id=spot(ahead(step)), device_id_type=MESH)
    pl.semaphore_wait(barrier, count - 1)
    first, second, tiny = [], [], []
    for step in range(1, count):
        target = ahead(step)
        if has_big:
            first.append(
                pltpu.make_async_remote_copy(
                    src_ref=big.at[target],
                    dst_ref=landed.at[step],
                    send_sem=send1.at[step],
                    recv_sem=recv1.at[step],
                    device_id=spot(target),
                    device_id_type=MESH,
                )
            )
            first[-1].start()
        if has_small:
            tiny.append(
                pltpu.make_async_remote_copy(
                    src_ref=small,
                    dst_ref=small_landed.at[step],
                    send_sem=send3.at[step],
                    recv_sem=recv3.at[step],
                    device_id=spot(target),
                    device_id_type=MESH,
                )
            )
            tiny[-1].start()
    if has_big:
        total = big[me]
        for step in range(1, count):
            first[step - 1].wait_recv()
            total = total + landed[step]
        out[me] = total
        for step in range(1, count):
            second.append(
                pltpu.make_async_remote_copy(
                    src_ref=out.at[me],
                    dst_ref=out.at[me],
                    send_sem=send2.at[step],
                    recv_sem=recv2.at[step],
                    device_id=spot(ahead(step)),
                    device_id_type=MESH,
                )
            )
            second[-1].start()
    if has_small:
        total = small[...]
        for step in range(1, count):
            tiny[step - 1].wait_recv()
            total = total + small_landed[step]
        small_out[...] = total
        for copy in tiny:
            copy.wait_send()
    if has_big:
        for copy in first:
            copy.wait_send()
        for step in range(1, count):
            source = lax.rem(me + count - step, count)
            pltpu.make_async_remote_copy(
                src_ref=out.at[source],
                dst_ref=out.at[source],
                send_sem=send2.at[step],
                recv_sem=recv2.at[step],
                device_id=spot(ahead(step)),
                device_id_type=MESH,
            ).wait_recv()
        for copy in second:
            copy.wait_send()


def total_over(big, small, collective_id):
    sections, shards = lax.axis_size("section"), lax.axis_size("shard")
    count = sections * shards
    rows = 8 * count if big is None else big.shape[0]
    if count > 16 or rows % (8 * count):
        given = tuple(part for part in (big, small) if part is not None)
        done = list(lax.psum(given, ("section", "shard")))
        return (
            done.pop(0) if big is not None else None,
            done.pop(0) if small is not None else None,
        )
    args, outs, scratch = [], [], []
    dma = pltpu.SemaphoreType.DMA((count,))
    if big is not None:
        shape = (count, rows // count, 128)
        args.append(big.reshape(shape))
        outs.append(jax.ShapeDtypeStruct(shape, jnp.float32))
        scratch += [pltpu.VMEM(shape, jnp.float32), dma, dma, dma, dma]
    if small is not None:
        args.append(small)
        outs.append(jax.ShapeDtypeStruct(small.shape, jnp.float32))
        scratch += [pltpu.VMEM((count,) + small.shape, jnp.float32), dma, dma]
    done = pl.pallas_call(
        functools.partial(reduce_kernel, sections, shards, big is not None, small is not None),
        out_shape=tuple(outs),
        in_specs=[pl.BlockSpec(memory_space=pltpu.VMEM)] * len(args),
        out_specs=tuple([pl.BlockSpec(memory_space=pltpu.VMEM)] * len(outs)),
        scratch_shapes=scratch,
        name="total_over_%d" % collective_id,
        compiler_params=pltpu.CompilerParams(collective_id=collective_id, has_side_effects=True),
    )(*args)
    done = list(done)
    return (
        done.pop(0).reshape(big.shape) if big is not None else None,
        done.pop(0) if small is not None else None,
    )


def scalars_tile(*values):
    row = jnp.stack(values)
    return jnp.pad(row[:, None], ((0, 8 - len(values)), (0, 127)))


def contract(a, b, axis_a, axis_b, split):
    dims = (((axis_a,), (axis_b,)), ((), ()))
    if not split:
        return lax.dot_general(a, b, dims, precision=PREC)

    def halves(x):
        high = x.astype(jnp.bfloat16)
        return high, (x - high.astype(jnp.float32)).astype(jnp.bfloat16)

    def mul(x, y):
        return lax.dot_general(x, y, dims, preferred_element_type=jnp.float32)

    (ah, al), (bh, bl) = halves(a), halves(b)
    return mul(ah, bh) + (mul(ah, bl) + mul(al, bh))


def pick(values, mask, rank):
    masked = values * mask
    count = masked.shape[1] // rank
    return sum(masked[:, k * rank : (k + 1) * rank] for k in range(count))


def spread(values, mask):
    count = mask.shape[1] // values.shape[1]
    return jnp.concatenate([values] * count, axis=1) * mask


def scale_low(raw, stats):
    rank = raw.shape[1] // 2
    recip = 1.0 / jnp.sqrt(stats[:, 0:1] / D + EPSILON)
    drift = -(recip * recip * recip) * stats[:, 1:2] / D
    low = raw[:, :rank] * (DOWN * recip)
    lowmove = (raw[:, rank:] * recip + raw[:, :rank] * drift) * DOWN
    return recip, low, lowmove


def step_up(split, raw, stats, mask, hidden, moving, up):
    wide = mask.shape[1]
    recip, low, lowmove = scale_low(raw, stats)
    spread_low = spread(UP * low, mask)
    fresh = hidden + contract(spread_low, up[:wide], 1, 0, split)
    move = contract(spread(UP * lowmove, mask), up[:wide], 1, 0, split)
    move = move + contract(spread_low, up[wide:], 1, 0, split)
    if moving is not None:
        move = move + moving
    return fresh, move, recip, low


def forward_step(has_moving, split, raw, stats, mask, hidden, *rest):
    moving, (up, down) = (rest[0], rest[1:]) if has_moving else (None, rest)
    wide, rank = mask.shape[1], raw.shape[1] // 2
    fresh, move, recip, low = step_up(split, raw, stats, mask, hidden, moving, up)
    first = contract(fresh, down[:wide], 1, 1, split)
    second = contract(fresh, down[wide:], 1, 1, split) + contract(move, down[:wide], 1, 1, split)
    raw_next = jnp.concatenate([pick(first, mask, rank), pick(second, mask, rank)], axis=1)
    squares = jnp.sum(fresh * fresh, axis=1, keepdims=True)
    products = jnp.sum(fresh * move, axis=1, keepdims=True)
    return fresh, move, recip, low, raw_next, jnp.concatenate([squares, products], axis=1)


def last_step(split, raw, stats, mask, weights, hidden, moving, up):
    wide, rank = mask.shape[1], raw.shape[1] // 2
    _, move, recip, low = step_up(split, raw, stats, mask, hidden, moving, up)
    cot = move * weights
    partial = pick(contract(cot, up[:wide], 1, 1, split), mask, rank) * UP
    return cot, recip, low, partial, jnp.sum(cot * move, axis=1, keepdims=True)


def backward_step(split, low_cot, low, recip, mask, cot, hidden, down, up_before):
    rank = low.shape[1]
    grad_up = contract(spread(UP * low, mask), cot, 0, 0, split)
    spread_cot = spread(low_cot * (DOWN * recip), mask)
    grad_down = contract(spread_cot, hidden, 0, 0, split)
    pull = recip * recip * jnp.sum(low_cot * low, axis=1, keepdims=True) / D
    fresh = cot + contract(spread_cot, down, 1, 0, split) - pull * hidden
    partial = pick(contract(fresh, up_before, 1, 1, split), mask, rank) * UP
    return grad_up, grad_down, fresh, partial


def run_local(function, part, shapes, *args):
    if part % 128:
        return function(False, *args)

    def kernel(*refs):
        values = function(True, *[ref[...] for ref in refs[: len(args)]])
        for ref, value in zip(refs[len(args) :], values):
            ref[...] = value

    vmem = pl.BlockSpec(memory_space=pltpu.VMEM)
    return pl.pallas_call(
        kernel,
        out_shape=tuple(jax.ShapeDtypeStruct(shape, jnp.float32) for shape in shapes),
        in_specs=[vmem] * len(args),
        out_specs=tuple([vmem] * len(shapes)),
        compiler_params=pltpu.CompilerParams(vmem_limit_bytes=40 * 1024 * 1024),
    )(*args)


def body(embed, gains, theta, iterate, residual, direction, token_task, loss_mask):
    section = lax.axis_index("section")
    sections = lax.axis_size("section")
    here, tasks = theta.shape[0], theta.shape[1]
    rank = theta.shape[3]
    layers = here * sections
    tokens, width = embed.shape
    part = width // sections
    wide = tasks * rank
    half = tokens // 2
    onehot = (token_task[:, None] == jnp.arange(tasks, dtype=jnp.int32)[None, :]).astype(
        jnp.float32
    )
    mask = jnp.repeat(onehot, rank, axis=1)
    weights = loss_mask.astype(jnp.float32)[:, None]

    def columns(value, block):
        return lax.dynamic_slice_in_dim(value, block * part, part, value.ndim - 1)

    local = {}
    for j in range(here):
        for side in range(2):
            both = jnp.concatenate(
                [theta[j, :, side].reshape(wide, width), direction[j, :, side].reshape(wide, width)]
            )
            local[j, side] = both * gains[j][None, :] if side == 0 else both

    order = [(0, 1)] + [(j, side) for j in range(1, here) for side in range(2)] + [(0, 0)]
    mats = {}
    for j, side in order:
        skip = 1 if (j, side) == (0, 0) else 0
        choices = [columns(local[j, side], section)]
        for k in range(1, sections):
            choices.append(
                lax.ppermute(
                    columns(local[j, side], lax.rem(section + k, sections)),
                    "section",
                    [(s, (s + k) % sections) for s in range(skip, sections)],
                )
            )
        for q in range(sections):
            away = lax.rem(section + sections - q, sections)
            mats[q * here + j, side] = lax.select_n(away, *choices)

    embedded = embed.astype(jnp.float32)
    hidden = columns(embedded, section)
    moving = None
    saved = []
    first = contract(embedded, local[0, 0], 1, 1, False)
    raw = jnp.concatenate(
        [pick(first[:, :wide], mask, rank), pick(first[:, wide:], mask, rank)], axis=1
    )
    raw = jnp.where(section == 0, raw, 0.0)
    squares = jnp.sum(hidden * hidden, axis=1, keepdims=True)
    stats = jnp.concatenate([squares, jnp.zeros_like(squares)], axis=1)
    square, tall = (tokens, part), (tokens, rank)
    one, two = (tokens, 1), (tokens, 2)
    for layer in range(layers):
        small = stats.T.reshape(8, -1)
        raw, small = total_over(raw, small, 0)
        stats = small.reshape(2, tokens).T
        if layer < layers - 1:
            given = (raw, stats, mask, hidden) + (() if moving is None else (moving,))
            fresh, move, recip, low, raw, stats = run_local(
                functools.partial(forward_step, moving is not None),
                part,
                (square, square, one, tall, (tokens, 2 * rank), two),
                *given,
                mats[layer, 1],
                mats[layer + 1, 0],
            )
            saved.append((hidden, recip, low))
            hidden, moving = fresh, move
        else:
            cot, recip, low, partial, curved = run_local(
                last_step,
                part,
                (square, one, tall, tall, one),
                raw, stats, mask, weights, hidden, moving, mats[layer, 1],
            )
            saved.append((hidden, recip, low))

    scalars = scalars_tile(
        jnp.sum(curved), jnp.sum(direction * direction), jnp.sum(residual * residual)
    )
    came = {}

    def send_home(layer, side, value):
        owner = layer // here
        parts = []
        for m in range(sections):
            parts.append(value if m == owner else lax.ppermute(value, "section", [(m, owner)]))
        came[layer, side] = parts

    for layer in reversed(range(layers)):
        hidden, recip, low = saved[layer]
        packed = jnp.concatenate([partial[:half], partial[half:]], axis=1)
        if layer == layers - 1:
            packed, summed = total_over(packed, scalars, 1)
            squared_old = summed[2, 0]
            alpha = squared_old / (summed[0, 0] + DAMPING_FACTOR * summed[1, 0])
        else:
            if layer == 0:
                send_home(0, 1, contract(spread(UP * low, mask), cot, 0, 0, False))
            packed, _ = total_over(packed, None, 2)
        low_cot = jnp.concatenate([packed[:, :rank], packed[:, rank:]])
        if layer == 0:
            spread_cot = spread(low_cot * (DOWN * recip), mask)
            first_down = contract(spread_cot, embedded, 0, 0, False)
        else:
            grad_up, grad_down, cot, partial = run_local(
                backward_step,
                part,
                ((wide, part), (wide, part), square, tall),
                low_cot, low, recip, mask, cot, hidden, mats[layer, 0][:wide], mats[layer - 1, 1][:wide],
            )
            send_home(layer, 0, grad_down)
            send_home(layer, 1, grad_up)

    product = []
    for j in range(here):
        for side in range(2):
            candidates = []
            for q in range(sections):
                layer = q * here + j
                if layer == 0 and side == 0:
                    candidates.append(first_down)
                else:
                    candidates.append(jnp.concatenate(came[layer, side], axis=1))
            full = lax.select_n(section, *candidates)
            product.append(full * gains[j][None, :] if side == 0 else full)
    gradient = jnp.stack(product).reshape(here, 2, tasks, rank, width).transpose(0, 2, 1, 3, 4)
    product = gradient + DAMPING_FACTOR * direction
    new_iterate = iterate + alpha * direction
    updated_residual_stream = residual - alpha * product
    _, summed = total_over(
        None, scalars_tile(jnp.sum(updated_residual_stream * updated_residual_stream)), 3
    )
    new_direction = updated_residual_stream + summed[0, 0] / squared_old * direction
    return (new_iterate, updated_residual_stream, new_direction)


def solution(mesh):
    spec = P("section", "groups", None, None, "shard")
    return jax.shard_map(
        body,
        mesh=mesh,
        in_specs=(
            P("groups", "shard"),
            P("section", "shard"),
            spec,
            spec,
            spec,
            spec,
            P("groups"),
            P("groups"),
        ),
        out_specs=(spec, spec, spec),
        check_vma=False,
    )
```
